32 devices in a mesh: groups: 2 (over x), gx: 4 (over y, core), gy: 4 (over z).
Axes of the slice: x: 2, y: 2, z: 4, core: 2. Of those that a mesh axis runs over, the one named last changes fastest.
Arguments:
- coarse_field: bfloat16 [64, 8, 16, 64], P('groups', 'gx', 'gy'), parts along dimension 0, may hold values from -6 to 6
- skip_field: bfloat16 [64, 16, 32, 128], P('groups', 'gx', 'gy'), parts along dimension 0, may hold values from -6 to 6
- cotangent: bfloat16 [64, 16, 32, 128], P('groups', 'gx', 'gy'), parts along dimension 0, may hold values from -6 to 6
- up_kernel: bfloat16 [32, 32, 3, 3, 3], replicated, may hold values from -0.5 to 0.5
- up_offset: float32 [32], replicated, may hold values from -2.5 to 2.5
- conv_kernel: bfloat16 [32, 64, 3, 3, 3], replicated, may hold values from -0.15625 to 0.15625
- conv_bias: float32 [32], replicated, may hold values from -2.5 to 2.5
Outputs:
- level_output: bfloat16 [64, 16, 32, 128], P('groups', 'gx', 'gy'), parts along dimension 0
- skip_grad: bfloat16 [64, 16, 32, 128], P('groups', 'gx', 'gy'), parts along dimension 0
- kernel_grad: float32 [64, 64, 3, 3, 3], P('groups'), parts along dimension 0
- bias_grad: float32 [64], P('groups'), parts along dimension 0
- up_grad: float32 [64, 32, 3, 3, 3], P('groups'), parts along dimension 0
- offset_grad: float32 [64], P('groups'), parts along dimension 0
The draws below stay inside these ranges and needn't reach their ends.
There are 2 independent parts, one for each index of `groups`. The reference program is written for one: setup_inputs(seed, part) draws one part's arguments, and reference() takes and returns one part's arrays. A program takes and returns all parts, laid end to end along the dimension named above; an argument that names none is the same for every part. Nothing has to cross between parts.
All inputs are finite; a program needn't handle non-finite values.
Results may differ from the reference program's by a relative error of at most 0.0049.
Values may be sent and summed in bfloat16 or wider, within the bound.
A program may use at most 64 MiB of HBM per device.

```python
import math
import jax
import jax.numpy as jnp
from jax import lax

CH = 32
NZ = 128
NX = 16
NY = 32


def shard_levels(stream_key, shape, cuts, least, largest):
    gain = 1.0
    for dim, blocks in cuts:
        steps = jax.random.uniform(jax.random.fold_in(jax.random.fold_in(stream_key, 6), dim), (blocks,), jnp.float32, least / len(cuts), largest / len(cuts))
        gain = gain * jnp.repeat(jnp.exp(steps), shape[dim] // blocks).reshape((-1,) + (1,) * (len(shape) - 1 - dim))
    return gain


def noise(key, dims, width, most, shards=(), kind=jnp.bfloat16):
    entries = jax.random.normal(key, dims, jnp.float32) * width
    if len(shards) > 0:
        entries = shard_levels(key, dims, shards, -0.22, 0.18) * entries
    return jnp.clip(entries, min=-most, max=most).astype(kind)


def setup_inputs(seed: int = 0, part: int = 0) -> dict:
    seeds = jax.random.split(jax.random.key(seed), 8)
    own_keys = jax.random.split(jax.random.fold_in(seeds[7], part), 8)
    coarse_field = noise(own_keys[0], (CH, NX // 2, NY // 2, NZ // 2), 1.0, 6.0, ((1, 4), (2, 4)))
    skip_field = noise(own_keys[1], (CH, NX, NY, NZ), 1.0, 6.0, ((1, 4), (2, 4)))
    cotangent = noise(own_keys[2], (CH, NX, NY, NZ), 1.0, 6.0, ((1, 4), (2, 4)))
    up_kernel = noise(seeds[3], (CH, CH, 3, 3, 3), (CH * 4) ** -0.5, 0.5)
    up_offset = noise(seeds[4], (CH,), 0.5, 2.5, (), jnp.float32)
    conv_kernel = noise(seeds[5], (CH, 2 * CH, 3, 3, 3), (54 * CH) ** -0.5, 0.15625)
    conv_bias = noise(seeds[6], (CH,), 0.5, 2.5, (), jnp.float32)
    return dict(coarse_field=coarse_field, skip_field=skip_field, cotangent=cotangent, up_kernel=up_kernel, up_offset=up_offset, conv_kernel=conv_kernel, conv_bias=conv_bias)


conv_layout = ('NCDHW', 'OIDHW', 'NCDHW')
highest = lax.Precision.HIGHEST

def wrap_along(volume, along, leading, trailing):
    extent = volume.shape[along]
    pieces = []
    if leading > 0:
        pieces.append(lax.slice_in_dim(volume, extent - leading, extent, axis=along))
    pieces.append(volume)
    if trailing > 0:
        pieces.append(lax.slice_in_dim(volume, 0, trailing, axis=along))
    return jnp.concatenate(pieces, axis=along)

def wrap_all(volume, leading, trailing):
    for along in (1, 2, 3):
        volume = wrap_along(volume, along, leading, trailing)
    return volume

def convolve(padded, kernel, padding, dilation):
    return lax.conv_general_dilated(padded[None], kernel, (1, 1, 1), padding, lhs_dilation=dilation, dimension_numbers=conv_layout, precision=highest, preferred_element_type=jnp.float32)[0]

def elu_of(preact):
    return jnp.where(preact > 0.0, preact, jnp.expm1(jnp.minimum(preact, 0.0)))

def slope_of(preact):
    return jnp.where(preact > 0.0, 1.0, jnp.exp(jnp.minimum(preact, 0.0)))

def reference(coarse_field, skip_field, cotangent, up_kernel, up_offset, conv_kernel, conv_bias):
    channels = skip_field.shape[0]
    scaling = 1.0 / math.sqrt(NX * NY * NZ)
    coarse_ext = wrap_all(coarse_field, 0, 1).astype(jnp.float32)
    flipped_up = up_kernel[:, :, ::-1, ::-1, ::-1].astype(jnp.float32)
    upsampled = convolve(coarse_ext, flipped_up, ((1, 0), (1, 0), (1, 0)), (2, 2, 2))
    upsampled = (upsampled + up_offset[:, None, None, None]).astype(jnp.bfloat16)
    joined = jnp.concatenate((upsampled, skip_field), axis=0)
    joined_ext = wrap_all(joined, 1, 1).astype(jnp.float32)
    kernel_full = conv_kernel.astype(jnp.float32)
    preact = convolve(joined_ext, kernel_full, ((0, 0), (0, 0), (0, 0)), (1, 1, 1)) + conv_bias[:, None, None, None]
    level_output = elu_of(preact).astype(jnp.bfloat16)
    grad_pre = (cotangent.astype(jnp.float32) * slope_of(preact)).astype(jnp.bfloat16)
    grad_ext = wrap_all(grad_pre, 1, 1).astype(jnp.float32)
    adjoint = jnp.transpose(kernel_full[:, :, ::-1, ::-1, ::-1], (1, 0, 2, 3, 4))
    joined_grad = convolve(grad_ext, adjoint, ((0, 0), (0, 0), (0, 0)), (1, 1, 1))
    skip_grad = joined_grad[channels:].astype(jnp.bfloat16)
    up_cot = joined_grad[:channels].astype(jnp.bfloat16)
    grad_rows = grad_pre.astype(jnp.float32).reshape(channels, -1)
    size_x, size_y, size_z = (grad_pre.shape[1], grad_pre.shape[2], grad_pre.shape[3])
    contract = (((1,), (1,)), ((), ()))
    tap_list = []
    for index_x in range(3):
        for index_y in range(3):
            for index_z in range(3):
                window = lax.slice(joined_ext, (0, index_x, index_y, index_z), (2 * channels, index_x + size_x, index_y + size_y, index_z + size_z))
                window = window.reshape(2 * channels, -1)
                tap_list.append(lax.dot_general(grad_rows, window, contract, precision=highest, preferred_element_type=jnp.float32))
    kernel_grad = jnp.stack(tap_list, axis=-1).reshape(channels, 2 * channels, 3, 3, 3) * scaling
    bias_grad = lax.optimization_barrier(jnp.sum(grad_pre.astype(jnp.float32), axis=(1, 2, 3))) * scaling
    cot_ext = wrap_all(up_cot, 1, 0).astype(jnp.float32)
    coarse_rows = coarse_field.astype(jnp.float32).reshape(channels, -1)
    count_x, count_y, count_z = (coarse_field.shape[1], coarse_field.shape[2], coarse_field.shape[3])
    lift_list = []
    for index_x in range(3):
        for index_y in range(3):
            for index_z in range(3):
                piece = lax.slice(cot_ext, (0, index_x, index_y, index_z), (channels, index_x + 2 * count_x - 1, index_y + 2 * count_y - 1, index_z + 2 * count_z - 1), (1, 2, 2, 2))
                piece = piece.reshape(channels, -1)
                lift_list.append(lax.dot_general(piece, coarse_rows, contract, precision=highest, preferred_element_type=jnp.float32))
    up_grad = jnp.stack(lift_list, axis=-1).reshape(channels, channels, 3, 3, 3) * scaling
    offset_grad = lax.optimization_barrier(jnp.sum(up_cot.astype(jnp.float32), axis=(1, 2, 3))) * scaling
    return (level_output, skip_grad, kernel_grad, bias_grad, up_grad, offset_grad)
```

```python
import functools
import math

import jax
import jax.numpy as jnp
from jax import lax
from jax.experimental import pallas as pl
from jax.experimental.pallas import tpu as pltpu
from jax.sharding import PartitionSpec as P

f32 = jnp.float32
bf16 = jnp.bfloat16


def halo(block, axis, dim, low_width, high_width):
    count = lax.axis_size(axis)
    forward = [(i, (i + 1) % count) for i in range(count)]
    backward = [((i + 1) % count, i) for i in range(count)]
    extent = block.shape[dim]
    low = lax.ppermute(
        lax.slice_in_dim(block, extent - low_width, None, axis=dim), axis, forward
    )
    high = lax.ppermute(lax.slice_in_dim(block, 0, high_width, axis=dim), axis, backward)
    return jnp.concatenate([low, block, high], axis=dim)


def mm(lhs, rhs):
    return jnp.dot(lhs, rhs, preferred_element_type=f32)


def mmt(lhs, rhs):
    return lax.dot_general(lhs, rhs, (((1,), (1,)), ((), ())), preferred_element_type=f32)


def roll(value, shift):
    return pltpu.roll(value, shift % value.shape[-1], value.ndim - 1)


def body(dims, scaling, coarse, skip, cot, wee, weo, woe, woo, wf, wa, uo, cb,
         lvl, sg, tot, dil, joi, gra, gr3, uc3, akg, aug, abg, aog):
    ch, nx, ny, nz = dims
    hx, hy = nx // 2, ny // 2
    wide = (hy + 2) * nz
    spread = (
        lax.broadcasted_iota(jnp.int32, (nz // 2, nz), 1)
        == 2 * lax.broadcasted_iota(jnp.int32, (nz // 2, nz), 0)
    ).astype(f32).astype(bf16)
    for q in range(hy + 3):
        thin = mm(coarse[q], spread).astype(bf16)
        for p in range(hx + 3):
            dil[p, :, q * nz : (q + 1) * nz] = thin[p * ch : (p + 1) * ch]

    offset = jnp.broadcast_to(uo[...], (ch, nz))
    weights = ((wee, weo), (woe, woo))

    @pl.loop(0, hx + 2)
    def _(p):
        for px in range(2):
            for py in range(2):
                rhs = jnp.concatenate(
                    [
                        dil[p + ia, :, ib * nz : ib * nz + wide]
                        for ia in range(1 + px)
                        for ib in range(1 + py)
                    ],
                    axis=0,
                )
                t = mm(weights[px][py][...], rhs)
                for m in range(hy + 2):
                    s = slice(m * nz, (m + 1) * nz)
                    row = (
                        roll(t[:ch, s], -1) + t[ch : 2 * ch, s] + roll(t[2 * ch :, s], 1)
                    ) + offset
                    y = 2 * m + py
                    joi[2 * p + px, :ch, y * nz : (y + 1) * nz] = row.astype(bf16)
            joi[2 * p + px, ch:, :] = skip[2 * p + px]

    bias = jnp.broadcast_to(cb[...], (ch, nz))
    abg[...] = jnp.zeros_like(abg)
    aog[...] = jnp.zeros_like(aog)
    akg[...] = jnp.zeros_like(akg)
    aug[...] = jnp.zeros_like(aug)

    def forward(x, own):
        span = (ny + 2) * nz
        rhs = jnp.concatenate(
            [joi[x + a, :, b * nz : b * nz + span] for a in range(3) for b in range(3)], axis=0
        )
        t = mm(wf[...], rhs)
        for y in range(ny + 2):
            s = slice(y * nz, (y + 1) * nz)
            v = roll(t[:ch, s], 1) + t[ch : 2 * ch, s] + roll(t[2 * ch :, s], -1) + bias
            e = jnp.exp(jnp.minimum(v, 0.0))
            g = (cot[x, :, s].astype(f32) * jnp.where(v > 0.0, 1.0, e)).astype(bf16)
            gra[x, :, s] = g
            if own and 1 <= y <= ny:
                d = slice((y - 1) * nz, y * nz)
                lvl[x - 1, :, d] = jnp.where(v > 0.0, v, e - 1.0).astype(bf16)
                g = g.astype(f32)
                abg[...] += g
                gr3[x - 1, :ch, d] = roll(g, -1).astype(bf16)
                gr3[x - 1, ch : 2 * ch, d] = g.astype(bf16)
                gr3[x - 1, 2 * ch :, d] = roll(g, 1).astype(bf16)

    @pl.loop(0, 2)
    def _(i):
        forward(i * (nx + 1), False)

    @pl.loop(0, nx)
    def _(x):
        forward(x + 1, True)

    @pl.loop(0, nx)
    def _(x):
        span = ny * nz
        lhs = jnp.concatenate(
            [
                joi[x + 1 + a, :, (1 + b) * nz : (1 + b) * nz + span]
                for a in range(3)
                for b in range(3)
            ],
            axis=0,
        )
        akg[...] += mmt(lhs, gr3[x])

    @pl.loop(0, nx)
    def _(x):
        span = ny * nz
        rhs = jnp.concatenate(
            [gra[x + a, :, b * nz : b * nz + span] for a in range(3) for b in range(3)], axis=0
        )
        t = mm(wa[...], rhs)
        w = 2 * ch
        for y in range(ny):
            s = slice(y * nz, (y + 1) * nz)
            j = roll(t[:w, s], -1) + t[w : 2 * w, s] + roll(t[2 * w :, s], 1)
            sg[x, :, s] = j[ch:].astype(bf16)
            u = j[:ch].astype(bf16).astype(f32)
            aog[...] += u
            at = (y % 2) * hy + y // 2
            d = slice(at * nz, (at + 1) * nz)
            uc3[x, :ch, d] = roll(u, 1).astype(bf16)
            uc3[x, ch : 2 * ch, d] = u.astype(bf16)
            uc3[x, 2 * ch :, d] = roll(u, -1).astype(bf16)

    half = hy * nz
    taps = (((1, 0),), ((2, 0), (0, 1)))

    @pl.loop(0, hx)
    def _(p):
        for px in range(2):
            for py in range(2):
                lhs = jnp.concatenate(
                    [
                        dil[p + 1 + da, :, (1 + db) * nz : (1 + db) * nz + half]
                        for a, da in taps[px]
                        for b, db in taps[py]
                    ],
                    axis=0,
                )
                r = mmt(lhs, uc3[2 * p + px, :, py * half : (py + 1) * half])
                k = 0
                for a, da in taps[px]:
                    for b, db in taps[py]:
                        at = (a * 3 + b) * ch
                        aug[at : at + ch, :] += r[k : k + ch]
                        k += ch

    kg = akg[...].T * scaling
    ug = aug[...].T * scaling
    for ab in range(9):
        for c in range(3):
            o = slice(c * ch, (c + 1) * ch)
            tot[ab * 3 + c, :, : 2 * ch] = kg[o, ab * 2 * ch : (ab + 1) * 2 * ch]
            tot[ab * 3 + c, :, 2 * ch : 3 * ch] = ug[o, ab * ch : (ab + 1) * ch]
            tot[ab * 3 + c, :, 3 * ch :] = jnp.zeros((ch, ch), f32)
    bsum = jnp.sum(abg[...], axis=1, keepdims=True) * scaling
    osum = jnp.sum(aog[...], axis=1, keepdims=True) * scaling
    tot[27, :, : 2 * ch] = jnp.broadcast_to(bsum, (ch, 2 * ch))
    tot[27, :, 2 * ch :] = jnp.broadcast_to(osum, (ch, 2 * ch))


def local(coarse_field, skip_field, cotangent, up_kernel, up_offset, conv_kernel, conv_bias):
    ch, nx, ny, nz = skip_field.shape
    hx, hy = nx // 2, ny // 2
    cells = nx * ny * nz * lax.axis_size("gx") * lax.axis_size("gy")
    scaling = 1.0 / math.sqrt(cells)

    skip = jnp.transpose(skip_field, (1, 0, 2, 3)).reshape(nx, ch, ny * nz)
    cot = jnp.transpose(cotangent, (1, 0, 2, 3)).reshape(nx, ch, ny * nz)
    skip = halo(halo(skip, "gx", 0, 2, 2), "gy", 2, 2 * nz, 2 * nz)
    cot = halo(halo(cot, "gx", 0, 1, 1), "gy", 2, nz, nz)
    coarse = jnp.transpose(coarse_field, (2, 1, 0, 3))
    coarse = halo(halo(coarse, "gx", 1, 1, 2), "gy", 0, 1, 2)
    coarse = coarse.reshape(hy + 3, (hx + 3) * ch, nz // 2)

    def up_weight(taps_a, taps_b):
        w = jnp.stack([up_kernel[:, :, a, b, :] for a in taps_a for b in taps_b], axis=-1)
        return jnp.transpose(w, (2, 0, 3, 1)).reshape(3 * ch, -1)

    ups = [up_weight(a, b) for a in ((1,), (2, 0)) for b in ((1,), (2, 0))]
    wf = jnp.transpose(conv_kernel, (4, 0, 2, 3, 1)).reshape(3 * ch, 18 * ch)
    wa = jnp.transpose(conv_kernel[:, :, ::-1, ::-1, :], (4, 1, 2, 3, 0)).reshape(6 * ch, 9 * ch)

    vmem = pl.BlockSpec(memory_space=pltpu.VMEM)
    lvl, sg, tot = pl.pallas_call(
        functools.partial(body, (ch, nx, ny, nz), scaling),
        out_shape=(
            jax.ShapeDtypeStruct((nx, ch, ny * nz), bf16),
            jax.ShapeDtypeStruct((nx, ch, ny * nz), bf16),
            jax.ShapeDtypeStruct((28, ch, 4 * ch), f32),
        ),
        in_specs=[vmem] * 11,
        out_specs=(vmem, vmem, vmem),
        scratch_shapes=[
            pltpu.VMEM((hx + 3, ch, (hy + 3) * nz), bf16),
            pltpu.VMEM((nx + 4, 2 * ch, (ny + 4) * nz), bf16),
            pltpu.VMEM((nx + 2, ch, (ny + 2) * nz), bf16),
            pltpu.VMEM((nx, 3 * ch, ny * nz), bf16),
            pltpu.VMEM((nx, 3 * ch, ny * nz), bf16),
            pltpu.VMEM((18 * ch, 3 * ch), f32),
            pltpu.VMEM((9 * ch, 3 * ch), f32),
            pltpu.VMEM((ch, nz), f32),
            pltpu.VMEM((ch, nz), f32),
        ],
        compiler_params=pltpu.CompilerParams(vmem_limit_bytes=48 << 20),
        name="level",
    )(coarse, skip, cot, *ups, wf, wa, up_offset[:, None], conv_bias[:, None])

    tot = lax.psum(tot, ("gx", "gy"))

    def unpack(v):
        return jnp.transpose(v.reshape(nx, ch, ny, nz), (1, 0, 2, 3))

    def kernel_of(v):
        return jnp.transpose(v.reshape(3, 3, 3, ch, -1), (3, 4, 0, 1, 2))

    return (
        unpack(lvl),
        unpack(sg),
        kernel_of(tot[:27, :, : 2 * ch]),
        tot[27, :, 0],
        kernel_of(tot[:27, :, 2 * ch : 3 * ch]),
        tot[27, :, 2 * ch],
    )


def solution(mesh):
    field = P("groups", "gx", "gy", None)
    kernel = P("groups", None, None, None, None)
    return jax.shard_map(
        local,
        mesh=mesh,
        in_specs=(field, field, field, P(), P(), P(), P()),
        out_specs=(field, field, kernel, P("groups"), kernel, P("groups")),
        check_vma=False,
    )
```

```python
import functools
import math

import jax
import jax.numpy as jnp
from jax import lax
from jax.experimental import pallas as pl
from jax.experimental.pallas import tpu as pltpu
from jax.sharding import PartitionSpec as P

f32 = jnp.float32
bf16 = jnp.bfloat16


def halo(block, axis, dim, low_width, high_width):
    count = lax.axis_size(axis)
    forward = [(i, (i + 1) % count) for i in range(count)]
    backward = [((i + 1) % count, i) for i in range(count)]
    extent = block.shape[dim]
    low = lax.ppermute(
        lax.slice_in_dim(block, extent - low_width, None, axis=dim), axis, forward
    )
    high = lax.ppermute(lax.slice_in_dim(block, 0, high_width, axis=dim), axis, backward)
    return jnp.concatenate([low, block, high], axis=dim)


def mm(lhs, rhs):
    return jnp.dot(lhs, rhs, preferred_element_type=f32)


def mmt(lhs, rhs):
    return lax.dot_general(lhs, rhs, (((1,), (1,)), ((), ())), preferred_element_type=f32)


def roll(value, shift):
    return pltpu.roll(value, shift % value.shape[-1], value.ndim - 1)


def body(dims, scaling, coarse, skip, cot, wee, weo, woe, woo, wf, wa, uo, cb,
         lvl, sg, tot, dil, joi, gra, gr3, uc3, akg, aug, abg, aog):
    ch, nx, ny, nz = dims
    hx, hy = nx // 2, ny // 2
    wide = (hy + 2) * nz
    spread = (
        lax.broadcasted_iota(jnp.int32, (nz // 2, nz), 1)
        == 2 * lax.broadcasted_iota(jnp.int32, (nz // 2, nz), 0)
    ).astype(f32).astype(bf16)
    for q in range(hy + 3):
        thin = mm(coarse[q], spread).astype(bf16)
        for p in range(hx + 3):
            dil[p, :, q * nz : (q + 1) * nz] = thin[p * ch : (p + 1) * ch]

    offset = jnp.broadcast_to(uo[...], (ch, nz))
    weights = ((wee, weo), (woe, woo))

    @pl.loop(0, hx + 2)
    def _(p):
        for px in range(2):
            for py in range(2):
                rhs = jnp.concatenate(
                    [
                        dil[p + ia, :, ib * nz : ib * nz + wide]
                        for ia in range(1 + px)
                        for ib in range(1 + py)
                    ],
                    axis=0,
                )
                t = mm(weights[px][py][...], rhs)
                for m in range(hy + 2):
                    s = slice(m * nz, (m + 1) * nz)
                    row = (
                        roll(t[:ch, s], -1) + t[ch : 2 * ch, s] + roll(t[2 * ch :, s], 1)
                    ) + offset
                    y = 2 * m + py
                    joi[2 * p + px, :ch, y * nz : (y + 1) * nz] = row.astype(bf16)
            joi[2 * p + px, ch:, :] = skip[2 * p + px]

    bias = jnp.broadcast_to(cb[...], (ch, nz))
    abg[...] = jnp.zeros_like(abg)
    aog[...] = jnp.zeros_like(aog)
    akg[...] = jnp.zeros_like(akg)
    aug[...] = jnp.zeros_like(aug)

    def forward(x, own):
        span = (ny + 2) * nz
        rhs = jnp.concatenate(
            [joi[x + a, :, b * nz : b * nz + span] for a in range(3) for b in range(3)], axis=0
        )
        t = mm(wf[...], rhs)
        for y in range(ny + 2):
            s = slice(y * nz, (y + 1) * nz)
            v = roll(t[:ch, s], 1) + t[ch : 2 * ch, s] + roll(t[2 * ch :, s], -1) + bias
            e = jnp.exp(jnp.minimum(v, 0.0))
            g = (cot[x, :, s].astype(f32) * jnp.where(v > 0.0, 1.0, e)).astype(bf16)
            gra[x, :, s] = g
            if own and 1 <= y <= ny:
                d = slice((y - 1) * nz, y * nz)
                lvl[x - 1, :, d] = jnp.where(v > 0.0, v, e - 1.0).astype(bf16)
                g = g.astype(f32)
                abg[...] += g
                gr3[x - 1, :ch, d] = roll(g, -1).astype(bf16)
                gr3[x - 1, ch : 2 * ch, d] = g.astype(bf16)
                gr3[x - 1, 2 * ch :, d] = roll(g, 1).astype(bf16)

    @pl.loop(0, 2)
    def _(i):
        forward(i * (nx + 1), False)

    @pl.loop(0, nx)
    def _(x):
        forward(x + 1, True)

    @pl.loop(0, nx)
    def _(x):
        span = ny * nz
        lhs = jnp.concatenate(
            [
                joi[x + 1 + a, :, (1 + b) * nz : (1 + b) * nz + span]
                for a in range(3)
                for b in range(3)
            ],
            axis=0,
        )
        akg[...] += mmt(lhs, gr3[x])

    @pl.loop(0, nx)
    def _(x):
        span = ny * nz
        rhs = jnp.concatenate(
            [gra[x + a, :, b * nz : b * nz + span] for a in range(3) for b in range(3)], axis=0
        )
        t = mm(wa[...], rhs)
        w = 2 * ch
        for y in range(ny):
            s = slice(y * nz, (y + 1) * nz)
            j = roll(t[:w, s], -1) + t[w : 2 * w, s] + roll(t[2 * w :, s], 1)
            sg[x, :, s] = j[ch:].astype(bf16)
            u = j[:ch].astype(bf16).astype(f32)
            aog[...] += u
            at = (y % 2) * hy + y // 2
            d = slice(at * nz, (at + 1) * nz)
            uc3[x, :ch, d] = roll(u, 1).astype(bf16)
            uc3[x, ch : 2 * ch, d] = u.astype(bf16)
            uc3[x, 2 * ch :, d] = roll(u, -1).astype(bf16)

    half = hy * nz
    taps = (((1, 0),), ((2, 0), (0, 1)))

    @pl.loop(0, hx)
    def _(p):
        for px in range(2):
            for py in range(2):
                lhs = jnp.concatenate(
                    [
                        dil[p + 1 + da, :, (1 + db) * nz : (1 + db) * nz + half]
                        for a, da in taps[px]
                        for b, db in taps[py]
                    ],
                    axis=0,
                )
                r = mmt(lhs, uc3[2 * p + px, :, py * half : (py + 1) * half])
                k = 0
                for a, da in taps[px]:
                    for b, db in taps[py]:
                        at = (a * 3 + b) * ch
                        aug[at : at + ch, :] += r[k : k + ch]
                        k += ch

    kg = akg[...].T * scaling
    ug = aug[...].T * scaling
    for ab in range(9):
        for c in range(3):
            o = slice(c * ch, (c + 1) * ch)
            d = slice((ab * 3 + c) * ch, (ab * 3 + c + 1) * ch)
            tot[d, : 2 * ch] = kg[o, ab * 2 * ch : (ab + 1) * 2 * ch]
            tot[d, 2 * ch : 3 * ch] = ug[o, ab * ch : (ab + 1) * ch]
            tot[d, 3 * ch :] = jnp.zeros((ch, ch), f32)
    tot[27 * ch :, :] = jnp.zeros((tot.shape[0] - 27 * ch, tot.shape[1]), f32)
    tot[27 * ch : 27 * ch + 1, :ch] = jnp.sum(abg[...].T, axis=0, keepdims=True) * scaling
    tot[27 * ch + 8 : 27 * ch + 9, :ch] = jnp.sum(aog[...].T, axis=0, keepdims=True) * scaling


def partners(axis):
    me, count = lax.axis_index(axis), lax.axis_size(axis)
    return me, [lax.rem(me + d, count) for d in range(1, count)]


def reduce_body(ch, part, kg, bg, ug, og, land_x, own, land_y, res, send, recv):
    me_x, to_x = partners("gx")
    me_y, to_y = partners("gy")
    barrier = pltpu.get_barrier_semaphore()
    for axis, to in (("gx", to_x), ("gy", to_y)):
        for i in to:
            pl.semaphore_signal(
                barrier, inc=1, device_id={axis: i}, device_id_type=pl.DeviceIdType.MESH
            )
    pl.semaphore_wait(barrier, len(to_x) + len(to_y))
    used = [0]

    def copy(src, dst, axis, i):
        k = used[0]
        used[0] += 1
        c = pltpu.make_async_remote_copy(
            src_ref=src,
            dst_ref=dst,
            send_sem=send.at[k],
            recv_sem=recv.at[k],
            device_id={axis: i},
            device_id_type=pl.DeviceIdType.MESH,
        )
        c.start()
        return c

    started = []

    def settle(copies):
        started.extend(copies)
        for c in copies:
            c.wait_recv()

    settle([copy(part.at[i], land_x.at[d], "gx", i) for d, i in enumerate(to_x)])
    total = part[me_x]
    for d in range(len(to_x)):
        total = total + land_x[d]
    own[...] = total
    settle([copy(own.at[j], land_y.at[d], "gy", j) for d, j in enumerate(to_y)])
    total = own[me_y]
    for d in range(len(to_y)):
        total = total + land_y[d]
    res[me_x, me_y] = total
    settle([copy(res.at[me_x, me_y], res.at[me_x, me_y], "gy", j) for j in to_y])
    settle([copy(res.at[me_x], res.at[me_x], "gx", i) for i in to_x])
    full = res[...].reshape(-1, res.shape[-1])
    taps = full[: 27 * ch].reshape(27, ch, -1)
    kg[...] = taps[:, :, : 2 * ch]
    ug[...] = taps[:, :, 2 * ch : 3 * ch]
    bg[...] = full[27 * ch : 27 * ch + 1, :ch]
    og[...] = full[27 * ch + 8 : 27 * ch + 9, :ch]
    for c in started:
        c.wait_send()


def all_sum(tot, ch):
    gx, gy = lax.axis_size("gx"), lax.axis_size("gy")
    rows, lanes = tot.shape[0] // (gx * gy), tot.shape[1]
    vmem = pl.BlockSpec(memory_space=pltpu.VMEM)
    copies = 2 * (gx - 1) + 2 * (gy - 1)
    return pl.pallas_call(
        functools.partial(reduce_body, ch),
        out_shape=(
            jax.ShapeDtypeStruct((27, ch, 2 * ch), f32),
            jax.ShapeDtypeStruct((1, ch), f32),
            jax.ShapeDtypeStruct((27, ch, ch), f32),
            jax.ShapeDtypeStruct((1, ch), f32),
        ),
        in_specs=[vmem],
        out_specs=(vmem,) * 4,
        scratch_shapes=[
            pltpu.VMEM((gx - 1, gy, rows, lanes), f32),
            pltpu.VMEM((gy, rows, lanes), f32),
            pltpu.VMEM((gy - 1, rows, lanes), f32),
            pltpu.VMEM((gx, gy, rows, lanes), f32),
            pltpu.SemaphoreType.DMA((copies,)),
            pltpu.SemaphoreType.DMA((copies,)),
        ],
        compiler_params=pltpu.CompilerParams(
            collective_id=1, has_side_effects=True, vmem_limit_bytes=32 << 20
        ),
        name="total",
    )(tot.reshape(gx, gy, rows, lanes))


def local(coarse_field, skip_field, cotangent, up_kernel, up_offset, conv_kernel, conv_bias):
    ch, nx, ny, nz = skip_field.shape
    hx, hy = nx // 2, ny // 2
    cells = nx * ny * nz * lax.axis_size("gx") * lax.axis_size("gy")
    scaling = 1.0 / math.sqrt(cells)

    skip = jnp.transpose(skip_field, (1, 0, 2, 3)).reshape(nx, ch, ny * nz)
    cot = jnp.transpose(cotangent, (1, 0, 2, 3)).reshape(nx, ch, ny * nz)
    skip = halo(halo(skip, "gx", 0, 2, 2), "gy", 2, 2 * nz, 2 * nz)
    cot = halo(halo(cot, "gx", 0, 1, 1), "gy", 2, nz, nz)
    coarse = jnp.transpose(coarse_field, (2, 1, 0, 3))
    coarse = halo(halo(coarse, "gx", 1, 1, 2), "gy", 0, 1, 2)
    coarse = coarse.reshape(hy + 3, (hx + 3) * ch, nz // 2)

    def up_weight(taps_a, taps_b):
        w = jnp.stack([up_kernel[:, :, a, b, :] for a in taps_a for b in taps_b], axis=-1)
        return jnp.transpose(w, (2, 0, 3, 1)).reshape(3 * ch, -1)

    ups = [up_weight(a, b) for a in ((1,), (2, 0)) for b in ((1,), (2, 0))]
    wf = jnp.transpose(conv_kernel, (4, 0, 2, 3, 1)).reshape(3 * ch, 18 * ch)
    wa = jnp.transpose(conv_kernel[:, :, ::-1, ::-1, :], (4, 1, 2, 3, 0)).reshape(6 * ch, 9 * ch)

    parts = lax.axis_size("gx") * lax.axis_size("gy")
    rows = 8 * parts * pl.cdiv(28 * ch, 8 * parts)
    vmem = pl.BlockSpec(memory_space=pltpu.VMEM)
    lvl, sg, tot = pl.pallas_call(
        functools.partial(body, (ch, nx, ny, nz), scaling),
        out_shape=(
            jax.ShapeDtypeStruct((nx, ch, ny * nz), bf16),
            jax.ShapeDtypeStruct((nx, ch, ny * nz), bf16),
            jax.ShapeDtypeStruct((rows, 4 * ch), f32),
        ),
        in_specs=[vmem] * 11,
        out_specs=(vmem, vmem, vmem),
        scratch_shapes=[
            pltpu.VMEM((hx + 3, ch, (hy + 3) * nz), bf16),
            pltpu.VMEM((nx + 4, 2 * ch, (ny + 4) * nz), bf16),
            pltpu.VMEM((nx + 2, ch, (ny + 2) * nz), bf16),
            pltpu.VMEM((nx, 3 * ch, ny * nz), bf16),
            pltpu.VMEM((nx, 3 * ch, ny * nz), bf16),
            pltpu.VMEM((18 * ch, 3 * ch), f32),
            pltpu.VMEM((9 * ch, 3 * ch), f32),
            pltpu.VMEM((ch, nz), f32),
            pltpu.VMEM((ch, nz), f32),
        ],
        compiler_params=pltpu.CompilerParams(vmem_limit_bytes=48 << 20),
        name="level",
    )(coarse, skip, cot, *ups, wf, wa, up_offset[:, None], conv_bias[:, None])

    kg, bg, ug, og = all_sum(tot, ch)

    def unpack(v):
        return jnp.transpose(v.reshape(nx, ch, ny, nz), (1, 0, 2, 3))

    def kernel_of(v):
        return jnp.transpose(v.reshape(3, 3, 3, ch, -1), (3, 4, 0, 1, 2))

    return (
        unpack(lvl),
        unpack(sg),
        kernel_of(kg),
        bg.reshape(ch),
        kernel_of(ug),
        og.reshape(ch),
    )


def solution(mesh):
    field = P("groups", "gx", "gy", None)
    kernel = P("groups", None, None, None, None)
    return jax.shard_map(
        local,
        mesh=mesh,
        in_specs=(field, field, field, P(), P(), P(), P()),
        out_specs=(field, field, kernel, P("groups"), kernel, P("groups")),
        check_vma=False,
    )
```

```python
import functools
import math

import jax
import jax.numpy as jnp
from jax import lax
from jax.experimental import pallas as pl
from jax.experimental.pallas import tpu as pltpu
from jax.sharding import PartitionSpec as P

f32 = jnp.float32
bf16 = jnp.bfloat16


def span(step, extent, low, high):
    if step > 0:
        return (extent - low, low), (0, low)
    if step < 0:
        return (0, high), (low + extent, high)
    return (0, extent), (low, extent)


def fetch_body(plans, *refs):
    count = len(plans)
    ins, exts, (send, recv) = refs[:count], refs[count : 2 * count], refs[2 * count :]
    steps = [(i, j) for i in (-1, 0, 1) for j in (-1, 0, 1) if (i, j) != (0, 0)]

    def device(step):
        place = {}
        for axis, d in zip(("gx", "gy"), step):
            size = lax.axis_size(axis)
            place[axis] = lax.rem(lax.axis_index(axis) + size + d, size)
        return place

    barrier = pltpu.get_barrier_semaphore()
    for step in steps:
        pl.semaphore_signal(
            barrier, inc=1, device_id=device(step), device_id_type=pl.DeviceIdType.MESH
        )
    pl.semaphore_wait(barrier, len(steps))
    copies = []
    for step in steps:
        for src, dst, plan in zip(ins, exts, plans):
            at_src, at_dst = [slice(None)] * len(src.shape), [slice(None)] * len(src.shape)
            for d, (dim, unit, low, high) in zip(step, plan):
                (s0, n0), (d0, n1) = span(d, src.shape[dim] // unit, low, high)
                at_src[dim] = pl.ds(s0 * unit, n0 * unit)
                at_dst[dim] = pl.ds(d0 * unit, n1 * unit)
            k = len(copies)
            copies.append(
                pltpu.make_async_remote_copy(
                    src_ref=src.at[tuple(at_src)],
                    dst_ref=dst.at[tuple(at_dst)],
                    send_sem=send.at[k],
                    recv_sem=recv.at[k],
                    device_id=device(step),
                    device_id_type=pl.DeviceIdType.MESH,
                )
            )
            copies[-1].start()
    for src, dst, plan in zip(ins, exts, plans):
        at = [slice(None)] * len(src.shape)
        for dim, unit, low, high in plan:
            at[dim] = slice(low * unit, low * unit + src.shape[dim])
        dst[tuple(at)] = src[...]
    for c in copies:
        c.wait_recv()
    for c in copies:
        c.wait_send()


def fetch(arrays, plans):
    vmem = pl.BlockSpec(memory_space=pltpu.VMEM)
    shapes = []
    for v, plan in zip(arrays, plans):
        shape = list(v.shape)
        for dim, unit, low, high in plan:
            shape[dim] += unit * (low + high)
        shapes.append(jax.ShapeDtypeStruct(tuple(shape), v.dtype))
    return pl.pallas_call(
        functools.partial(fetch_body, plans),
        out_shape=tuple(shapes),
        in_specs=[vmem] * len(arrays),
        out_specs=(vmem,) * len(arrays),
        scratch_shapes=[pltpu.SemaphoreType.DMA((8 * len(arrays),))] * 2,
        compiler_params=pltpu.CompilerParams(
            collective_id=0, has_side_effects=True, vmem_limit_bytes=24 << 20
        ),
        name="fetch",
    )(*arrays)


def mm(lhs, rhs):
    return jnp.dot(lhs, rhs, preferred_element_type=f32)


def mmt(lhs, rhs):
    return lax.dot_general(lhs, rhs, (((1,), (1,)), ((), ())), preferred_element_type=f32)


def roll(value, shift):
    return pltpu.roll(value, shift % value.shape[-1], value.ndim - 1)


def body(dims, scaling, coarse, skip, cot, wee, weo, woe, woo, wf, wa, uo, cb,
         lvl, sg, tot, dil, joi, gra, gr3, uc3, akg, aug, abg, aog):
    ch, nx, ny, nz = dims
    hx, hy = nx // 2, ny // 2
    wide = (hy + 2) * nz
    spread = (
        lax.broadcasted_iota(jnp.int32, (nz // 2, nz), 1)
        == 2 * lax.broadcasted_iota(jnp.int32, (nz // 2, nz), 0)
    ).astype(f32).astype(bf16)
    for q in range(hy + 3):
        thin = mm(coarse[q], spread).astype(bf16)
        for p in range(hx + 3):
            dil[p, :, q * nz : (q + 1) * nz] = thin[p * ch : (p + 1) * ch]

    offset = jnp.broadcast_to(uo[...], (ch, nz))
    weights = ((wee, weo), (woe, woo))

    @pl.loop(0, hx + 2)
    def _(p):
        for px in range(2):
            for py in range(2):
                rhs = jnp.concatenate(
                    [
                        dil[p + ia, :, ib * nz : ib * nz + wide]
                        for ia in range(1 + px)
                        for ib in range(1 + py)
                    ],
                    axis=0,
                )
                t = mm(weights[px][py][...], rhs)
                for m in range(hy + 2):
                    s = slice(m * nz, (m + 1) * nz)
                    row = (
                        roll(t[:ch, s], -1) + t[ch : 2 * ch, s] + roll(t[2 * ch :, s], 1)
                    ) + offset
                    y = 2 * m + py
                    joi[2 * p + px, :ch, y * nz : (y + 1) * nz] = row.astype(bf16)
            joi[2 * p + px, ch:, :] = skip[2 * p + px]

    bias = jnp.broadcast_to(cb[...], (ch, nz))
    abg[...] = jnp.zeros_like(abg)
    aog[...] = jnp.zeros_like(aog)
    akg[...] = jnp.zeros_like(akg)
    aug[...] = jnp.zeros_like(aug)

    def forward(x, own):
        span = (ny + 2) * nz
        rhs = jnp.concatenate(
            [joi[x + a, :, b * nz : b * nz + span] for a in range(3) for b in range(3)], axis=0
        )
        t = mm(wf[...], rhs)
        for y in range(ny + 2):
            s = slice(y * nz, (y + 1) * nz)
            v = roll(t[:ch, s], 1) + t[ch : 2 * ch, s] + roll(t[2 * ch :, s], -1) + bias
            e = jnp.exp(jnp.minimum(v, 0.0))
            g = (cot[x, :, s].astype(f32) * jnp.where(v > 0.0, 1.0, e)).astype(bf16)
            gra[x, :, s] = g
            if own and 1 <= y <= ny:
                d = slice((y - 1) * nz, y * nz)
                lvl[x - 1, :, d] = jnp.where(v > 0.0, v, e - 1.0).astype(bf16)
                g = g.astype(f32)
                abg[...] += g
                gr3[x - 1, :ch, d] = roll(g, -1).astype(bf16)
                gr3[x - 1, ch : 2 * ch, d] = g.astype(bf16)
                gr3[x - 1, 2 * ch :, d] = roll(g, 1).astype(bf16)

    @pl.loop(0, 2)
    def _(i):
        forward(i * (nx + 1), False)

    @pl.loop(0, nx)
    def _(x):
        forward(x + 1, True)

    @pl.loop(0, nx)
    def _(x):
        span = ny * nz
        lhs = jnp.concatenate(
            [
                joi[x + 1 + a, :, (1 + b) * nz : (1 + b) * nz + span]
                for a in range(3)
                for b in range(3)
            ],
            axis=0,
        )
        akg[...] += mmt(lhs, gr3[x])

    @pl.loop(0, nx)
    def _(x):
        span = ny * nz
        rhs = jnp.concatenate(
            [gra[x + a, :, b * nz : b * nz + span] for a in range(3) for b in range(3)], axis=0
        )
        t = mm(wa[...], rhs)
        w = 2 * ch
        for y in range(ny):
            s = slice(y * nz, (y + 1) * nz)
            j = roll(t[:w, s], -1) + t[w : 2 * w, s] + roll(t[2 * w :, s], 1)
            sg[x, :, s] = j[ch:].astype(bf16)
            u = j[:ch].astype(bf16).astype(f32)
            aog[...] += u
            at = (y % 2) * hy + y // 2
            d = slice(at * nz, (at + 1) * nz)
            uc3[x, :ch, d] = roll(u, 1).astype(bf16)
            uc3[x, ch : 2 * ch, d] = u.astype(bf16)
            uc3[x, 2 * ch :, d] = roll(u, -1).astype(bf16)

    half = hy * nz
    taps = (((1, 0),), ((2, 0), (0, 1)))

    @pl.loop(0, hx)
    def _(p):
        for px in range(2):
            for py in range(2):
                lhs = jnp.concatenate(
                    [
                        dil[p + 1 + da, :, (1 + db) * nz : (1 + db) * nz + half]
                        for a, da in taps[px]
                        for b, db in taps[py]
                    ],
                    axis=0,
                )
                r = mmt(lhs, uc3[2 * p + px, :, py * half : (py + 1) * half])
                k = 0
                for a, da in taps[px]:
                    for b, db in taps[py]:
                        at = (a * 3 + b) * ch
                        aug[at : at + ch, :] += r[k : k + ch]
                        k += ch

    kg = akg[...].T * scaling
    ug = aug[...].T * scaling
    for ab in range(9):
        for c in range(3):
            o = slice(c * ch, (c + 1) * ch)
            d = slice((ab * 3 + c) * ch, (ab * 3 + c + 1) * ch)
            tot[d, : 2 * ch] = kg[o, ab * 2 * ch : (ab + 1) * 2 * ch]
            tot[d, 2 * ch : 3 * ch] = ug[o, ab * ch : (ab + 1) * ch]
            tot[d, 3 * ch :] = jnp.zeros((ch, ch), f32)
    tot[27 * ch :, :] = jnp.zeros((tot.shape[0] - 27 * ch, tot.shape[1]), f32)
    tot[27 * ch : 27 * ch + 1, :ch] = jnp.sum(abg[...].T, axis=0, keepdims=True) * scaling
    tot[27 * ch + 8 : 27 * ch + 9, :ch] = jnp.sum(aog[...].T, axis=0, keepdims=True) * scaling


def partners(axis):
    me, count = lax.axis_index(axis), lax.axis_size(axis)
    return me, [lax.rem(me + d, count) for d in range(1, count)]


def reduce_body(ch, part, kg, bg, ug, og, land_x, own, land_y, res, send, recv):
    me_x, to_x = partners("gx")
    me_y, to_y = partners("gy")
    barrier = pltpu.get_barrier_semaphore()
    for axis, to in (("gx", to_x), ("gy", to_y)):
        for i in to:
            pl.semaphore_signal(
                barrier, inc=1, device_id={axis: i}, device_id_type=pl.DeviceIdType.MESH
            )
    pl.semaphore_wait(barrier, len(to_x) + len(to_y))
    used = [0]

    def copy(src, dst, axis, i):
        k = used[0]
        used[0] += 1
        c = pltpu.make_async_remote_copy(
            src_ref=src,
            dst_ref=dst,
            send_sem=send.at[k],
            recv_sem=recv.at[k],
            device_id={axis: i},
            device_id_type=pl.DeviceIdType.MESH,
        )
        c.start()
        return c

    started = []

    def settle(copies):
        started.extend(copies)
        for c in copies:
            c.wait_recv()

    settle([copy(part.at[i], land_x.at[d], "gx", i) for d, i in enumerate(to_x)])
    total = part[me_x]
    for d in range(len(to_x)):
        total = total + land_x[d]
    own[...] = total
    settle([copy(own.at[j], land_y.at[d], "gy", j) for d, j in enumerate(to_y)])
    total = own[me_y]
    for d in range(len(to_y)):
        total = total + land_y[d]
    res[me_x, me_y] = total
    settle([copy(res.at[me_x, me_y], res.at[me_x, me_y], "gy", j) for j in to_y])
    settle([copy(res.at[me_x], res.at[me_x], "gx", i) for i in to_x])
    full = res[...].reshape(-1, res.shape[-1])
    taps = full[: 27 * ch].reshape(27, ch, -1)
    kg[...] = taps[:, :, : 2 * ch]
    ug[...] = taps[:, :, 2 * ch : 3 * ch]
    bg[...] = full[27 * ch : 27 * ch + 1, :ch]
    og[...] = full[27 * ch + 8 : 27 * ch + 9, :ch]
    for c in started:
        c.wait_send()


def all_sum(tot, ch):
    gx, gy = lax.axis_size("gx"), lax.axis_size("gy")
    rows, lanes = tot.shape[0] // (gx * gy), tot.shape[1]
    vmem = pl.BlockSpec(memory_space=pltpu.VMEM)
    copies = 2 * (gx - 1) + 2 * (gy - 1)
    return pl.pallas_call(
        functools.partial(reduce_body, ch),
        out_shape=(
            jax.ShapeDtypeStruct((27, ch, 2 * ch), f32),
            jax.ShapeDtypeStruct((1, ch), f32),
            jax.ShapeDtypeStruct((27, ch, ch), f32),
            jax.ShapeDtypeStruct((1, ch), f32),
        ),
        in_specs=[vmem],
        out_specs=(vmem,) * 4,
        scratch_shapes=[
            pltpu.VMEM((gx - 1, gy, rows, lanes), f32),
            pltpu.VMEM((gy, rows, lanes), f32),
            pltpu.VMEM((gy - 1, rows, lanes), f32),
            pltpu.VMEM((gx, gy, rows, lanes), f32),
            pltpu.SemaphoreType.DMA((copies,)),
            pltpu.SemaphoreType.DMA((copies,)),
        ],
        compiler_params=pltpu.CompilerParams(
            collective_id=1, has_side_effects=True, vmem_limit_bytes=32 << 20
        ),
        name="total",
    )(tot.reshape(gx, gy, rows, lanes))


def local(coarse_field, skip_field, cotangent, up_kernel, up_offset, conv_kernel, conv_bias):
    ch, nx, ny, nz = skip_field.shape
    hx, hy = nx // 2, ny // 2
    cells = nx * ny * nz * lax.axis_size("gx") * lax.axis_size("gy")
    scaling = 1.0 / math.sqrt(cells)

    skip = jnp.transpose(skip_field, (1, 0, 2, 3)).reshape(nx, ch, ny * nz)
    cot = jnp.transpose(cotangent, (1, 0, 2, 3)).reshape(nx, ch, ny * nz)
    coarse = jnp.transpose(coarse_field, (2, 1, 0, 3))
    skip, cot, coarse = fetch(
        (skip, cot, coarse),
        (
            ((0, 1, 2, 2), (2, nz, 2, 2)),
            ((0, 1, 1, 1), (2, nz, 1, 1)),
            ((1, 1, 1, 2), (0, 1, 1, 2)),
        ),
    )
    coarse = coarse.reshape(hy + 3, (hx + 3) * ch, nz // 2)

    def up_weight(taps_a, taps_b):
        w = jnp.stack([up_kernel[:, :, a, b, :] for a in taps_a for b in taps_b], axis=-1)
        return jnp.transpose(w, (2, 0, 3, 1)).reshape(3 * ch, -1)

    ups = [up_weight(a, b) for a in ((1,), (2, 0)) for b in ((1,), (2, 0))]
    wf = jnp.transpose(conv_kernel, (4, 0, 2, 3, 1)).reshape(3 * ch, 18 * ch)
    wa = jnp.transpose(conv_kernel[:, :, ::-1, ::-1, :], (4, 1, 2, 3, 0)).reshape(6 * ch, 9 * ch)

    parts = lax.axis_size("gx") * lax.axis_size("gy")
    rows = 8 * parts * pl.cdiv(28 * ch, 8 * parts)
    vmem = pl.BlockSpec(memory_space=pltpu.VMEM)
    lvl, sg, tot = pl.pallas_call(
        functools.partial(body, (ch, nx, ny, nz), scaling),
        out_shape=(
            jax.ShapeDtypeStruct((nx, ch, ny * nz), bf16),
            jax.ShapeDtypeStruct((nx, ch, ny * nz), bf16),
            jax.ShapeDtypeStruct((rows, 4 * ch), f32),
        ),
        in_specs=[vmem] * 11,
        out_specs=(vmem, vmem, vmem),
        scratch_shapes=[
            pltpu.VMEM((hx + 3, ch, (hy + 3) * nz), bf16),
            pltpu.VMEM((nx + 4, 2 * ch, (ny + 4) * nz), bf16),
            pltpu.VMEM((nx + 2, ch, (ny + 2) * nz), bf16),
            pltpu.VMEM((nx, 3 * ch, ny * nz), bf16),
            pltpu.VMEM((nx, 3 * ch, ny * nz), bf16),
            pltpu.VMEM((18 * ch, 3 * ch), f32),
            pltpu.VMEM((9 * ch, 3 * ch), f32),
            pltpu.VMEM((ch, nz), f32),
            pltpu.VMEM((ch, nz), f32),
        ],
        compiler_params=pltpu.CompilerParams(vmem_limit_bytes=48 << 20),
        name="level",
    )(coarse, skip, cot, *ups, wf, wa, up_offset[:, None], conv_bias[:, None])

    kg, bg, ug, og = all_sum(tot, ch)

    def unpack(v):
        return jnp.transpose(v.reshape(nx, ch, ny, nz), (1, 0, 2, 3))

    def kernel_of(v):
        return jnp.transpose(v.reshape(3, 3, 3, ch, -1), (3, 4, 0, 1, 2))

    return (
        unpack(lvl),
        unpack(sg),
        kernel_of(kg),
        bg.reshape(ch),
        kernel_of(ug),
        og.reshape(ch),
    )


def solution(mesh):
    field = P("groups", "gx", "gy", None)
    kernel = P("groups", None, None, None, None)
    return jax.shard_map(
        local,
        mesh=mesh,
        in_specs=(field, field, field, P(), P(), P(), P()),
        out_specs=(field, field, kernel, P("groups"), kernel, P("groups")),
        check_vma=False,
    )
```
